512 devices in a mesh: row: 16 (over x_hi, y, core), col: 32 (over x_lo, z).
Axes of the slice: x: 4 (x_hi: 2, x_lo: 2; x = x_hi * 2 + x_lo), y: 4, z: 16, core: 2. Of those that a mesh axis runs over, the one named last changes fastest.
Arguments:
- blocks: bfloat16 [1536, 64, 4096], P('col', 'row'), may hold values from -1.75 to 1.75
- columns: int32 [1536, 64], P('col', 'row'), may hold values from 0 to 95, as said below
- counts: int32 [1536, 16], P('col', 'row'), may hold values from 0 to 4, as said below
Outputs:
- product: bfloat16 [1536, 64, 4096], P('col', 'row')
The draws below stay inside these ranges and needn't reach their ends.
Inputs may be any that keep to these rules, and one draw needn't show every extreme that they name: `counts`: in each tile, every block row has between 0 and 4 live slots; in every tile some block row has exactly 4. The live slots of a block row name different tile columns, at most 2 of them below 48 and at most 2 at or above; in every tile some block row reaches 2 in both halves. A live tile column t of global block row g satisfies (t - g) mod 48 < 8. Dead slots hold arbitrary values in the range.
All inputs are finite; a program needn't handle non-finite values.
Results may differ from the reference program's by a relative error of at most 0.001.
Values may be sent and summed in bfloat16 or wider, within the bound.
No kernel may reach another device: no remote copies, remote signals or barrier semaphores. Data moves between devices by JAX's collectives and lax.ppermute only.
A program may use at most 128 MiB of HBM per device.

```python
import jax
import jax.numpy as jnp
from jax import lax

BLK = 64
HS = 2
BAND = 8
SECTIONS = 2
SLOTS = 4
NB = 1536
WB = 48
BB = 4096
N_ROW = 16
N_COL = 32


def pattern(key):
    keys = jax.random.split(jax.random.fold_in(key, 7), 9)
    first_count = jax.random.randint(keys[0], (NB, N_ROW), 0, HS + 1)
    second_count = jax.random.randint(keys[1], (NB, N_ROW), 0, HS + 1)
    pick = jax.random.randint(keys[2], (NB // WB, N_ROW), 0, WB)
    strip_pos = (jnp.arange(NB, dtype=jnp.int32) % WB)[:, None]
    filled = strip_pos == jnp.repeat(pick, WB, axis=0)
    first_count = jnp.where(filled, HS, first_count)
    second_count = jnp.where(filled, HS, second_count)
    global_row = jnp.arange(NB, dtype=jnp.int32)[:, None, None]
    member = jnp.arange(HS, dtype=jnp.int32)[None, None, :]
    first_base = jax.random.randint(keys[3], (NB, N_ROW, 1), 0, BAND)
    first_step = 2 * jax.random.randint(keys[4], (NB, N_ROW, 1), 0, BAND // 2) + 1
    second_base = jax.random.randint(keys[5], (NB, N_ROW, 1), 0, BAND)
    second_step = 2 * jax.random.randint(keys[6], (NB, N_ROW, 1), 0, BAND // 2) + 1
    first_cols = (global_row + (first_base + member * first_step) % BAND) % WB
    second_cols = WB + (global_row + (second_base + member * second_step) % BAND) % WB
    slot_ids = jnp.arange(SLOTS, dtype=jnp.int32)[None, None, :]
    fc = first_count[:, :, None]
    sc = second_count[:, :, None]
    first_take = jnp.take_along_axis(first_cols, jnp.clip(slot_ids, 0, HS - 1) * jnp.ones_like(fc), axis=2)
    second_take = jnp.take_along_axis(second_cols, jnp.clip(slot_ids - fc, 0, HS - 1), axis=2)
    garbage = jax.random.randint(keys[7], (NB, N_ROW, SLOTS), 0, 2 * WB)
    listed = jnp.where(slot_ids < fc, first_take, jnp.where(slot_ids < fc + sc, second_take, garbage))
    total = first_count + second_count
    scores = jax.random.randint(keys[8], (NB, N_ROW, SLOTS), 0, 2 ** 20) * 8 + slot_ids
    scores = jnp.where(slot_ids < total[:, :, None], scores, 2 ** 28 + slot_ids)
    order = jnp.argsort(scores, axis=-1, stable=True)
    listed = jnp.take_along_axis(listed, order, axis=-1)
    return (listed.reshape(NB, N_ROW * SLOTS).astype(jnp.int32), total.astype(jnp.int32))


def draw_columns(key, part):
    return pattern(key)[0]


def draw_counts(key, part):
    return pattern(key)[1]


def steps_of(key, dims, pieces, low, top_value):
    def one(dim, blocks):
        draws = jax.random.uniform(jax.random.fold_in(jax.random.fold_in(key, 6), dim), (blocks,), jnp.float32, low / len(pieces), top_value / len(pieces))
        return jnp.repeat(jnp.exp(draws), dims[dim] // blocks).reshape((-1,) + (1,) * (len(dims) - dim - 1))

    loudness = one(*pieces[0])
    for cut in pieces[1:]:
        loudness = loudness * one(*cut)
    return loudness


def centred(rng, extent, deviation, bound, cuts=(), held_as=jnp.bfloat16):
    values = deviation * jax.random.normal(rng, extent, jnp.float32)
    if cuts:
        values = values * steps_of(rng, extent, cuts, -0.22, 0.18)
    return jnp.clip(values, -bound, bound).astype(held_as)


def setup_inputs(seed: int = 0) -> dict:
    streams_of = jax.random.split(jax.random.key(seed), 4)
    return {
        "blocks": centred(streams_of[0], (NB, N_ROW * SLOTS, BB), 0.3, 1.75, ((0, 32), (1, 16))),
        "columns": draw_columns(jax.random.fold_in(streams_of[3], 71), 0),
        "counts": draw_counts(jax.random.fold_in(streams_of[3], 71), 0),
    }


def compact(tile_blocks, tile_cols, tile_count, half_index):
    strip_count = tile_cols.shape[0]
    slot_count = tile_cols.shape[1]
    slot_ids = jnp.arange(slot_count, dtype=jnp.int32)
    live_slots = (slot_ids[None, :] < tile_count[:, None]) & (tile_cols // strip_count == half_index)
    position = jnp.cumsum(live_slots.astype(jnp.int32), axis=1) - 1
    chosen = live_slots[:, :, None] & (position[:, :, None] == jnp.arange(HS, dtype=jnp.int32)[None, None, :])
    picked = jnp.einsum('isq,isx->iqx', chosen.astype(jnp.float32), tile_blocks.astype(jnp.float32)).astype(jnp.bfloat16)
    inner_rows = jnp.sum(jnp.where(chosen, (tile_cols - half_index * strip_count)[:, :, None], 0), axis=1).astype(jnp.int32)
    used_flags = jnp.any(chosen, axis=1).astype(jnp.int32)
    return picked, inner_rows, used_flags


def section_term(picked, inner_rows, used_flags, right_blocks, right_cols, right_count, out_cols, out_live):
    strip_count = picked.shape[0]
    slot_count = out_cols.shape[1]
    gathered = right_blocks[inner_rows]
    gathered_cols = right_cols[inner_rows]
    gathered_count = right_count[inner_rows]
    slot_ids = jnp.arange(slot_count, dtype=jnp.int32)
    right_live = slot_ids[None, None, :] < gathered_count[:, :, None]
    matches = (gathered_cols[:, :, :, None] == out_cols[:, None, None, :]) & right_live[:, :, :, None]
    matches = matches & (used_flags[:, :, None, None] > 0) & out_live[:, None, None, :]
    selected = jnp.einsum('iqbj,iqbx->iqjx', matches.astype(jnp.float32), gathered.astype(jnp.float32)).astype(jnp.bfloat16)
    left_blocks = picked.reshape(strip_count, HS, BLK, BLK).astype(jnp.float32)
    right_sel = selected.reshape(strip_count, HS, slot_count, BLK, BLK).astype(jnp.float32)
    contribution = jnp.einsum('iqmn,iqjnp->ijmp', left_blocks, right_sel)
    return contribution.reshape(strip_count, slot_count, BLK * BLK)


def reference(blocks, columns, counts):
    def take(piece, owner):
        start_row = (piece * WB).astype(jnp.int32)
        start_slot = (owner * SLOTS).astype(jnp.int32)
        zero_index = jnp.int32(0)
        tile_blocks = lax.dynamic_slice(blocks, (start_row, start_slot, zero_index), (WB, SLOTS, BB))
        tile_cols = lax.dynamic_slice(columns, (start_row, start_slot), (WB, SLOTS))
        tile_count = lax.dynamic_slice(counts, (start_row, owner.astype(jnp.int32)), (WB, 1))[:, 0]
        return tile_blocks, tile_cols, tile_count

    def one_device(device):
        col_id = (device // N_ROW).astype(jnp.int32)
        row_id = (device % N_ROW).astype(jnp.int32)
        own_blocks, own_cols, own_count = take(col_id, row_id)
        out_live = jnp.arange(SLOTS, dtype=jnp.int32)[None, :] < own_count[:, None]
        accumulated = jnp.zeros((WB, SLOTS, BB), jnp.float32)
        for section in range(SECTIONS):
            target_piece = ((col_id + section) % N_COL).astype(jnp.int32)
            root_index = (target_piece // 2).astype(jnp.int32)
            half_index = (target_piece % 2).astype(jnp.int32)
            left_tile = take(col_id, root_index)
            picked, inner_rows, used_flags = compact(left_tile[0], left_tile[1], left_tile[2], half_index)
            right_tile = take(target_piece, row_id)
            accumulated = accumulated + section_term(picked, inner_rows, used_flags, right_tile[0], right_tile[1], right_tile[2], own_cols, out_live)
        return accumulated.astype(jnp.bfloat16)

    tiles = lax.map(one_device, jnp.arange(N_COL * N_ROW, dtype=jnp.int32))
    tiles = tiles.reshape(N_COL, N_ROW, WB, SLOTS, BB).transpose(0, 2, 1, 3, 4)
    return tiles.reshape(NB, N_ROW * SLOTS, BB)
```

```python
import functools

import jax
import jax.numpy as jnp
from jax import lax
from jax.experimental import pallas as pl
from jax.experimental.pallas import tpu as pltpu
from jax.sharding import PartitionSpec as P

HALF = 2
SUB = 32
LANES = 128
LEFT = 32


def prep_kernel(hA_ref, cols_ref, counts_ref, tile_ref, ga_ref, gb_ref, om_ref, flat, index):
    rows = tile_ref.shape[0]
    slots = tile_ref.shape[1]
    tiles = tile_ref.shape[2] // LANES
    first = hA_ref[0]
    lane = lax.broadcasted_iota(jnp.int32, (1, LANES), 1)
    ga_ref[rows:] = jnp.zeros((ga_ref.shape[0] - rows,) + ga_ref.shape[1:], ga_ref.dtype)
    gb_ref[rows:] = jnp.zeros((gb_ref.shape[0] - rows,) + gb_ref.shape[1:], gb_ref.dtype)
    index[...] = jnp.zeros(index.shape, index.dtype)

    def row(i, _):
        buf = lax.rem(i, 2)
        count = counts_ref[0, i]
        used = [jnp.int32(0), jnp.int32(0)]
        at = [jnp.int32(0)] * (2 * HALF)
        col = [jnp.int32(-1)] * (2 * HALF)
        out_row = jnp.full((1, LANES), -1, jnp.int32)
        for j in range(slots):
            c = cols_ref[j, i]
            live = j < count
            second = (c >= rows).astype(jnp.int32)
            side = jnp.where(second == first, 0, 1)
            for x in range(2):
                here = live & (side == x)
                for k in range(HALF):
                    take = here & (used[x] == k)
                    at[x * HALF + k] = jnp.where(take, j, at[x * HALF + k])
                    col[x * HALF + k] = jnp.where(take, c, col[x * HALF + k])
                used[x] = used[x] + here.astype(jnp.int32)
            out_row = jnp.where(
                (lane < 16) & ((lane & 3) == j), jnp.where(live, c + 1, -1), out_row
            )
        om_ref[pl.ds(i, 1), :] = out_row.astype(jnp.float32)
        idx_row = jnp.zeros((1, LANES), jnp.int32)
        for r in range(2 * HALF):
            inner = jnp.where(col[r] >= rows, col[r] - rows, col[r])
            idx_row = jnp.where((lane < 16) & ((lane >> 2) == r), col[r] + 1, idx_row)
            idx_row = jnp.where(lane == LEFT + r, jnp.where(col[r] < 0, 255, inner), idx_row)
        index[pl.ds(i, 1), :] = idx_row.astype(jnp.float32)
        v = tile_ref[i].astype(jnp.float32)
        for t in range(tiles):
            flat[buf, pl.ds(slots * t, slots), :] = v[:, t * LANES : (t + 1) * LANES]
        for r in range(2 * HALF):
            x = flat[buf, pl.ds(at[r], SUB, stride=slots), :].astype(ga_ref.dtype)
            dst = ga_ref if r < HALF else gb_ref
            dst[i, r % HALF] = x
        return 0

    lax.fori_loop(0, rows, row, 0)
    packed = index[...].astype(ga_ref.dtype)
    for dst in (ga_ref, gb_ref):
        for k in range(HALF):
            dst[rows, k] = packed[k * SUB : (k + 1) * SUB]


def prep(first, cols_t, counts_t, tile):
    rows, slots, size = tile.shape
    pad = rows + 2
    half = jax.ShapeDtypeStruct((pad, HALF, SUB, LANES), tile.dtype)
    smem = pl.BlockSpec(memory_space=pltpu.SMEM)
    vmem = pl.BlockSpec(memory_space=pltpu.VMEM)
    return pl.pallas_call(
        prep_kernel,
        out_shape=(half, half, jax.ShapeDtypeStruct((rows, LANES), jnp.float32)),
        in_specs=[smem, smem, smem, vmem],
        out_specs=(vmem, vmem, vmem),
        scratch_shapes=[
            pltpu.VMEM((2, slots * size // LANES, LANES), jnp.float32),
            pltpu.VMEM((HALF * SUB, LANES), jnp.float32),
        ],
        compiler_params=pltpu.CompilerParams(vmem_limit_bytes=24 << 20),
        name="prep",
    )(first, cols_t, counts_t, tile)


def multiply_kernel(
    sec_ref, om_ref, ga, gb, za, zb, hf, ho, out_ref, right, left, table, tsm, acc, wide, sems, tsem
):
    rows = out_ref.shape[0]
    slots = out_ref.shape[1]
    tiles = out_ref.shape[2] // LANES
    copies = [
        pltpu.make_async_copy(src, dst, sems.at[n])
        for n, (src, dst) in enumerate(
            (
                (ga, right.at[0]),
                (gb, right.at[1]),
                (za, right.at[2]),
                (zb, right.at[3]),
                (hf, left.at[0]),
                (ho, left.at[1]),
            )
        )
    ]
    for c in copies:
        c.start()
    sec = sec_ref[0]
    lane = lax.broadcasted_iota(jnp.int32, (rows, LANES), 1)
    low = lax.broadcasted_iota(jnp.int32, (2 * SUB, LANES), 1) < LANES // 2
    weight = jnp.zeros((rows, LANES), jnp.float32)
    for r in range(2 * HALF):
        weight = jnp.where((lane >> 2) == r, ((lane & 3) + 1).astype(jnp.float32) * 8.0**r, weight)
    weight = jnp.where(lane < 16, weight, 0.0)
    for c in copies:
        c.wait()
    found = jnp.zeros((rows, LANES), jnp.float32)
    total = jnp.zeros((rows, 1), jnp.float32)
    om = om_ref[...]
    for x in range(2):
        s = sec if x == 0 else 1 - sec
        rm = jnp.concatenate([right[2 * s, rows, k] for k in range(HALF)], 0)
        lm = jnp.concatenate([left[x, rows, k] for k in range(HALF)], 0)[:rows].astype(jnp.float32)
        for k in range(HALF):
            e = jnp.sum(jnp.where(lane == LEFT + 2 * s + k, lm, 0.0), axis=1, keepdims=True)
            pick = (lane[:, : HALF * SUB].astype(jnp.float32) == e).astype(rm.dtype)
            got = jnp.dot(pick, rm, preferred_element_type=jnp.float32)
            code = jnp.sum(jnp.where(got == om, weight, 0.0), axis=1, keepdims=True)
            found = jnp.where(lane == x * HALF + k, code, found)
            found = jnp.where(lane == 8 + x * HALF + k, e, found)
            total = total + code
    found = jnp.where(lane == 4, total, found)
    table[...] = found.astype(jnp.int32)
    put = pltpu.make_async_copy(table, tsm, tsem)
    put.start()
    put.wait()

    def row(i, _):
        any_match = tsm[i, 4]

        @pl.when(any_match == 0)
        def _():
            out_ref[i] = jnp.zeros(out_ref.shape[1:], out_ref.dtype)

        @pl.when(any_match != 0)
        def _():
            acc[...] = jnp.zeros(acc.shape, acc.dtype)
            for x in range(2):
                s = sec if x == 0 else 1 - sec
                for k in range(HALF):
                    code = tsm[i, x * HALF + k]

                    @pl.when(code != 0)
                    def _(x=x, k=k, s=s, code=code):
                        e = tsm[i, 8 + x * HALF + k]

                        def slot(r, _):
                            j = lax.shift_right_logical(code, 3 * r) & 7

                            @pl.when(j != 0)
                            def _():
                                b = right[2 * s + lax.shift_right_logical(r, 1), e, r & 1]
                                b = b.astype(jnp.float32)
                                wide[pl.ds(0, SUB, stride=2), :] = b
                                wide[pl.ds(1, SUB, stride=2), :] = pltpu.roll(b, LANES // 2, 1)
                                w = wide[...]
                                diag = jnp.concatenate(
                                    [
                                        jnp.where(low, w, 0.0),
                                        jnp.where(low, 0.0, pltpu.roll(w, LANES // 2, 1)),
                                    ],
                                    0,
                                ).astype(left.dtype)
                                got = jnp.dot(
                                    left[x, i, k], diag, preferred_element_type=jnp.float32
                                )
                                at = pl.ds(j - 1, SUB, stride=slots)
                                acc[at, :] = acc[at, :] + got

                            return 0

                        lax.fori_loop(0, 2 * HALF, slot, 0)

            for t in range(tiles):
                out_ref[i, :, t * LANES : (t + 1) * LANES] = acc[
                    pl.ds(slots * t, slots), :
                ].astype(out_ref.dtype)

        return 0

    lax.fori_loop(0, rows, row, 0)


def multiply(sec, om, ga, gb, za, zb, hf, ho, slots):
    rows = om.shape[0]
    size = 2 * SUB * SUB * 2
    hbm = pl.BlockSpec(memory_space=pl.ANY)
    vmem = pl.BlockSpec(memory_space=pltpu.VMEM)
    return pl.pallas_call(
        multiply_kernel,
        out_shape=jax.ShapeDtypeStruct((rows, slots, size), ga.dtype),
        in_specs=[pl.BlockSpec(memory_space=pltpu.SMEM), vmem] + [hbm] * 6,
        out_specs=vmem,
        scratch_shapes=[
            pltpu.VMEM((4,) + ga.shape, ga.dtype),
            pltpu.VMEM((2,) + ga.shape, ga.dtype),
            pltpu.VMEM((rows, LANES), jnp.int32),
            pltpu.SMEM((rows, LANES), jnp.int32),
            pltpu.VMEM((slots * size // LANES, LANES), jnp.float32),
            pltpu.VMEM((2 * SUB, LANES), jnp.float32),
            pltpu.SemaphoreType.DMA((6,)),
            pltpu.SemaphoreType.DMA,
        ],
        compiler_params=pltpu.CompilerParams(vmem_limit_bytes=32 << 20),
        name="multiply",
    )(sec, om, ga, gb, za, zb, hf, ho)


def local(blocks, columns, counts, n_row, n_col):
    slots = columns.shape[1]
    p = lax.axis_index("col")
    q = lax.axis_index("row")
    k = p // 2
    even = p % 2 == 0
    root_a = k
    root_b = jnp.where(even, k ^ 1, (k + 1) % n_row)
    in_a = (q & 1) == (root_a & 1)
    root = jnp.where(in_a, root_a, root_b)
    role = (((q >> 1) & 3) - ((root >> 1) & 3)) % 4

    ga, gb, om = prep((p % 2).reshape(1).astype(jnp.int32), columns.T, counts.T, blocks)

    to_a, to_b, to_core = [], [], []
    for c in range(n_col):
        owner_a = c // 2
        owner_b = owner_a if c % 2 == 0 else (owner_a + 1) % n_row
        tree_b = owner_b ^ 1 if c % 2 == 0 else owner_b
        to_a.append((owner_a * n_col + c, (owner_a ^ 8) * n_col + c))
        to_b.append((owner_b * n_col + c, (tree_b ^ 8) * n_col + c))
        if owner_b != tree_b:
            to_core.append((owner_b * n_col + c, tree_b * n_col + c))
    both = ("row", "col")
    from_next = [((i + 1) % n_col, i) for i in range(n_col)]

    def along_y(v, d):
        route = [(i, (i & ~6) | ((((i >> 1) & 3) + d) % 4) << 1) for i in range(n_row)]
        return lax.ppermute(v, "row", route)

    got_a = lax.ppermute(ga, both, to_a)
    got_b = lax.ppermute(gb, both, to_b)
    got_core = lax.ppermute(gb, both, to_core)
    za = lax.ppermute(ga, "col", from_next)
    got_a, got_b, got_core, za = lax.optimization_barrier((got_a, got_b, got_core, za))
    start = jnp.where(q == root_a, ga, jnp.where((q == root_b) & ~even, gb, got_a + got_b + got_core))
    mid = start.shape[0] // 2
    a, b = start[:mid], start[mid:]
    top = role == 0
    up = along_y(a, 1)
    down = along_y(b, -1)
    up, down = lax.optimization_barrier((up, down))
    up2 = along_y(jnp.where(top, b, up), 1)
    down2 = along_y(jnp.where(top, a, down), -1)
    zb = lax.ppermute(gb, "col", from_next)
    up2, down2, zb = lax.optimization_barrier((up2, down2, zb))
    half_a = jnp.where(top, a, jnp.where(role == 1, up, jnp.where(role == 3, down2, up2)))
    half_b = jnp.where(top, b, jnp.where(role == 1, up2, jnp.where(role == 3, down, down2)))
    mine = jnp.concatenate([half_a, half_b], 0)
    other = lax.ppermute(mine, "row", [(i, i ^ 1) for i in range(n_row)])
    sec = jnp.where(in_a, 0, 1).reshape(1).astype(jnp.int32)
    return multiply(sec, om, ga, gb, za, zb, mine, other, slots)


def solution(mesh):
    step = functools.partial(local, n_row=mesh.shape["row"], n_col=mesh.shape["col"])
    return jax.shard_map(
        step,
        mesh=mesh,
        in_specs=(P("col", "row", None), P("col", "row"), P("col", "row")),
        out_specs=P("col", "row", None),
        check_vma=False,
    )
```

```python
import functools

import jax
import jax.numpy as jnp
from jax import lax
from jax.experimental import pallas as pl
from jax.experimental.pallas import tpu as pltpu
from jax.sharding import PartitionSpec as P

HALF = 2
SUB = 32
LANES = 128
AHEAD = 4
FIRST, WHICH, ROLE, HEAD, LAST, SECTION = range(6)
CROSS = 35
LEFT = 32
VMEM = pl.BlockSpec(memory_space=pltpu.VMEM)
SMEM = pl.BlockSpec(memory_space=pltpu.SMEM)


def prep_kernel(flags, table, tile, g, om_ref, flat, index):
    rows, slots, size = tile.shape
    tiles = size // LANES
    first = flags[FIRST]
    lane = lax.broadcasted_iota(jnp.int32, (1, LANES), 1)
    g[:, rows:] = jnp.zeros((2, g.shape[1] - rows) + g.shape[2:], g.dtype)
    index[...] = jnp.zeros(index.shape, index.dtype)

    def row(i, _):
        buf = lax.rem(i, 2)
        count = table[slots, i]
        used = [jnp.int32(0), jnp.int32(0)]
        at = [jnp.int32(0)] * (2 * HALF)
        col = [jnp.int32(-1)] * (2 * HALF)
        out_row = jnp.full((1, LANES), -1, jnp.int32)
        for j in range(slots):
            c = table[j, i]
            live = j < count
            second = (c >= rows).astype(jnp.int32)
            side = jnp.where(second == first, 0, 1)
            for x in range(2):
                here = live & (side == x)
                for k in range(HALF):
                    take = here & (used[x] == k)
                    at[x * HALF + k] = jnp.where(take, j, at[x * HALF + k])
                    col[x * HALF + k] = jnp.where(take, c, col[x * HALF + k])
                used[x] = used[x] + here.astype(jnp.int32)
            out_row = jnp.where(
                (lane < 16) & ((lane & 3) == j), jnp.where(live, c + 1, -1), out_row
            )
        om_ref[pl.ds(i, 1), :] = out_row.astype(jnp.float32)
        idx_row = jnp.zeros((1, LANES), jnp.int32)
        for r in range(2 * HALF):
            inner = jnp.where(col[r] >= rows, col[r] - rows, col[r])
            idx_row = jnp.where((lane < 16) & ((lane >> 2) == r), col[r] + 1, idx_row)
            idx_row = jnp.where(lane == LEFT + r, jnp.where(col[r] < 0, 255, inner), idx_row)
        index[pl.ds(i, 1), :] = idx_row.astype(jnp.float32)
        v = tile[i].astype(jnp.float32)
        for t in range(tiles):
            flat[buf, pl.ds(slots * t, slots), :] = v[:, t * LANES : (t + 1) * LANES]
        for r in range(2 * HALF):
            x = flat[buf, pl.ds(at[r], SUB, stride=slots), :].astype(g.dtype)
            g[r // HALF, i, r % HALF] = x
        return 0

    lax.fori_loop(0, rows, row, 0)
    packed = index[...].astype(g.dtype)
    for x in range(2):
        for k in range(HALF):
            g[x, rows, k] = packed[k * SUB : (k + 1) * SUB]


def prep(flags, table, tile):
    rows, slots, size = tile.shape
    return pl.pallas_call(
        prep_kernel,
        out_shape=(
            jax.ShapeDtypeStruct((2, rows + 2, HALF, SUB, LANES), tile.dtype),
            jax.ShapeDtypeStruct((rows, LANES), jnp.float32),
        ),
        in_specs=[SMEM, SMEM, VMEM],
        out_specs=(VMEM, VMEM),
        scratch_shapes=[
            pltpu.VMEM((2, slots * size // LANES, LANES), jnp.float32),
            pltpu.VMEM((HALF * SUB, LANES), jnp.float32),
        ],
        compiler_params=pltpu.CompilerParams(vmem_limit_bytes=12 << 20),
        name="prep",
    )(flags, table, tile)


def pick_kernel(flags, *refs):
    *sources, tile, a, b, whole, cross = refs
    mid = a.shape[0]
    for n, src in enumerate(sources):

        @pl.when(flags[WHICH] == n)
        def _(src=src):
            a[...] = src[:mid]
            b[...] = src[mid:]

    @pl.when(flags[HEAD] != 0)
    def _():
        rest = tile.shape[1] - CROSS
        whole[: tile.shape[1]] = tile[0]
        whole[tile.shape[1] :] = tile[1, :rest]
        cross[...] = tile[1, rest:]


def pick(flags, tile, *sources):
    shape = tile.shape[1:]
    piece = lambda n: jax.ShapeDtypeStruct((n,) + shape[1:], tile.dtype)
    return pl.pallas_call(
        pick_kernel,
        out_shape=(
            piece(shape[0] // 2),
            piece(shape[0] // 2),
            piece(2 * shape[0] - CROSS),
            piece(CROSS),
        ),
        in_specs=[SMEM] + [VMEM] * (len(sources) + 1),
        out_specs=(VMEM,) * 4,
        compiler_params=pltpu.CompilerParams(vmem_limit_bytes=4 << 20),
        name="pick",
    )(flags, *sources, tile)


def turn_kernel(flags, a, b, up, down, c, d):
    role = flags[ROLE]

    @pl.when(role == 0)
    def _():
        c[...] = b[...]
        d[...] = a[...]

    @pl.when(role == 1)
    def _():
        c[...] = up[...]

    @pl.when(role == 3)
    def _():
        d[...] = down[...]


def turn(flags, *pieces):
    piece = jax.ShapeDtypeStruct(pieces[0].shape, pieces[0].dtype)
    return pl.pallas_call(
        turn_kernel,
        out_shape=(piece, piece),
        in_specs=[SMEM] + [VMEM] * len(pieces),
        out_specs=(VMEM, VMEM),
        compiler_params=pltpu.CompilerParams(vmem_limit_bytes=4 << 20),
        name="turn",
    )(flags, *pieces)


def join_kernel(flags, *refs):
    *pieces, wrap, cross, behind, out, right = refs
    mid = pieces[0].shape[0]
    for role in range(4):

        @pl.when(flags[ROLE] == role)
        def _(role=role):
            out[:mid] = pieces[2 * role][...]
            out[mid:] = pieces[2 * role + 1][...]

    @pl.when(flags[LAST] != 0)
    def _():
        rest = right.shape[1] - CROSS
        right[0] = wrap[: right.shape[1]]
        right[1, :rest] = wrap[right.shape[1] :]
        right[1, rest:] = cross[...]


def join(flags, wrap, cross, behind, *pieces):
    shape = pieces[0].shape
    return pl.pallas_call(
        join_kernel,
        out_shape=(
            jax.ShapeDtypeStruct((2 * shape[0],) + shape[1:], pieces[0].dtype),
            jax.ShapeDtypeStruct(behind.shape, behind.dtype),
        ),
        in_specs=[SMEM] + [VMEM] * (len(pieces) + 3),
        out_specs=(VMEM, VMEM),
        input_output_aliases={len(pieces) + 3: 1},
        compiler_params=pltpu.CompilerParams(vmem_limit_bytes=4 << 20),
        name="join",
    )(flags, *pieces, wrap, cross, behind)


def multiply_kernel(
    flags, om_ref, own, behind, mine, other, out_ref, table, tsm, todo, acc, wide, tsem
):
    rows, slots, size = out_ref.shape
    tiles = size // LANES
    sec = flags[SECTION]
    lane = lax.broadcasted_iota(jnp.int32, (rows, LANES), 1)
    low = lax.broadcasted_iota(jnp.int32, (2 * SUB, LANES), 1) < LANES // 2
    weight = jnp.zeros((rows, LANES), jnp.float32)
    for r in range(2 * HALF):
        weight = jnp.where((lane >> 2) == r, ((lane & 3) + 1).astype(jnp.float32) * 8.0**r, weight)
    weight = jnp.where(lane < 16, weight, 0.0)
    found = jnp.zeros((rows, LANES), jnp.float32)
    total = jnp.zeros((rows, 1), jnp.float32)
    om = om_ref[...]
    for s in range(2):
        right = own if s == 0 else behind
        rm = jnp.concatenate([right[0, rows, k] for k in range(HALF)], 0)
        lm = [
            jnp.concatenate([left[rows, k] for k in range(HALF)], 0)[:rows].astype(jnp.float32)
            for left in (mine, other)
        ]
        lm = jnp.where(sec == s, lm[0], lm[1])
        for k in range(HALF):
            e = jnp.sum(jnp.where(lane == LEFT + HALF * s + k, lm, 0.0), axis=1, keepdims=True)
            pick = (lane[:, : HALF * SUB].astype(jnp.float32) == e).astype(rm.dtype)
            got = jnp.dot(pick, rm, preferred_element_type=jnp.float32)
            code = jnp.sum(jnp.where(got == om, weight, 0.0), axis=1, keepdims=True)
            found = jnp.where(lane == s * HALF + k, code, found)
            found = jnp.where(lane == 8 + s * HALF + k, e, found)
            total = total + code
    found = jnp.where(lane == 4, total, found)
    table[...] = found.astype(jnp.int32)
    put = pltpu.make_async_copy(table, tsm, tsem)
    put.start()
    put.wait()

    def scan(i, n):
        def some(n):
            acc[i] = jnp.zeros(acc.shape[1:], acc.dtype)
            for c in range(2 * HALF):
                code = tsm[i, c]
                base = (i << 16) | (tsm[i, 8 + c] << 8) | (c << 5)
                for r in range(2 * HALF):
                    j = lax.shift_right_logical(code, 3 * r) & 7
                    todo[n] = base | (r << 3) | (j - 1)
                    n = n + (j != 0).astype(jnp.int32)
            return n

        return lax.cond(tsm[i, 4] != 0, some, lambda n: n, n)

    n_todo = lax.fori_loop(0, rows, scan, jnp.int32(0))
    for u in range(AHEAD):
        todo[n_todo + u] = rows << 16
    acc[rows] = jnp.zeros(acc.shape[1:], acc.dtype)

    def pairs(m, _):
        items = []
        for u in range(AHEAD):
            w = todo[m * AHEAD + u]
            i = lax.shift_right_logical(w, 16)
            e = lax.shift_right_logical(w, 8) & 63
            s = lax.shift_right_logical(w, 6) & 1
            k = lax.shift_right_logical(w, 5) & 1
            x = lax.shift_right_logical(w, 4) & 1
            h = lax.shift_right_logical(w, 3) & 1
            b = jnp.where(s == 0, own[x, e, h].astype(jnp.float32), behind[x, e, h].astype(jnp.float32))
            a = jnp.where(sec == s, mine[i, k].astype(jnp.float32), other[i, k].astype(jnp.float32))
            wide[u, pl.ds(0, SUB, stride=2), :] = b
            wide[u, pl.ds(1, SUB, stride=2), :] = pltpu.roll(b, LANES // 2, 1)
            items.append((i, w & 3, a.astype(mine.dtype)))
        sums = []
        for u, (_, _, a) in enumerate(items):
            v = wide[u]
            diag = jnp.concatenate(
                [jnp.where(low, v, 0.0), jnp.where(low, 0.0, pltpu.roll(v, LANES // 2, 1))], 0
            ).astype(mine.dtype)
            sums.append(jnp.dot(a, diag, preferred_element_type=jnp.float32))
        for (i, j, _), got in zip(items, sums):
            at = pl.ds(j, SUB, stride=slots)
            acc[i, at, :] = acc[i, at, :] + got
        return 0

    lax.fori_loop(0, (n_todo + AHEAD - 1) // AHEAD, pairs, 0)

    def finish(i, _):
        @pl.when(tsm[i, 4] == 0)
        def _():
            out_ref[i] = jnp.zeros(out_ref.shape[1:], out_ref.dtype)

        @pl.when(tsm[i, 4] != 0)
        def _():
            for t in range(tiles):
                out_ref[i, :, t * LANES : (t + 1) * LANES] = acc[
                    i, pl.ds(slots * t, slots), :
                ].astype(out_ref.dtype)

        return 0

    lax.fori_loop(0, rows, finish, 0)


def multiply(flags, om, own, behind, mine, other, slots):
    rows = om.shape[0]
    size = 2 * SUB * SUB * 2
    return pl.pallas_call(
        multiply_kernel,
        out_shape=jax.ShapeDtypeStruct((rows, slots, size), own.dtype),
        in_specs=[SMEM] + [VMEM] * 5,
        out_specs=VMEM,
        scratch_shapes=[
            pltpu.VMEM((rows, LANES), jnp.int32),
            pltpu.SMEM((rows, LANES), jnp.int32),
            pltpu.SMEM((rows * 4 * HALF * HALF + 2 * AHEAD,), jnp.int32),
            pltpu.VMEM((rows + 1, slots * size // LANES, LANES), jnp.float32),
            pltpu.VMEM((AHEAD, 2 * SUB, LANES), jnp.float32),
            pltpu.SemaphoreType.DMA,
        ],
        compiler_params=pltpu.CompilerParams(vmem_limit_bytes=12 << 20),
        name="multiply",
    )(flags, om, own, behind, mine, other)


def routes(n_row, n_col):
    to_a, to_b, to_core = [], [], []
    up, down, up_on, down_on = [], [], [], []
    for c in range(n_col):
        owner_a = c // 2
        owner_b = owner_a if c % 2 == 0 else (owner_a + 1) % n_row
        tree_b = owner_b ^ 1 if c % 2 == 0 else owner_b
        rank = lambda q: q * n_col + c
        to_a.append((rank(owner_a), rank(owner_a ^ 8)))
        to_b.append((rank(owner_b), rank(tree_b ^ 8)))
        if owner_b != tree_b:
            to_core.append((rank(owner_b), rank(tree_b)))
        for root in (owner_a, tree_b):
            for x in (0, 8):
                y = (root >> 1) & 3
                at = lambda d: rank((root & 8) ^ x | ((y + d) & 3) << 1 | root & 1)
                up.append((at(0), at(1)))
                down.append((at(0), at(3)))
                up_on.append((at(1), at(2)))
                down_on.append((at(3), at(2)))
    return to_a, to_b, to_core, up, down, up_on, down_on


def local(blocks, columns, counts, n_row, n_col):
    slots = columns.shape[1]
    p = lax.axis_index("col")
    q = lax.axis_index("row")
    k = p // 2
    even = p % 2 == 0
    root_a = k
    root_b = jnp.where(even, k ^ 1, (k + 1) % n_row)
    in_a = (q & 1) == (root_a & 1)
    root = jnp.where(in_a, root_a, root_b)
    role = (((q >> 1) & 3) - ((root >> 1) & 3)) & 3
    which = jnp.where(
        in_a,
        jnp.where(q == root_a, 0, 2),
        jnp.where(q == root_b, jnp.where(even, 4, 1), 3),
    )
    which = jnp.where(role == 0, which, -1)
    n_z = n_col // 2
    last = lambda i: (i + 1) % n_z == 0
    flags = [p % 2, which, role, p % n_z == 0, last(p), jnp.where(in_a, 0, 1)]
    flags = jnp.stack([v.astype(jnp.int32) for v in flags])

    table = jnp.concatenate([columns.T, counts.T], 0)
    tile, om = prep(flags, table, blocks)
    ga, gb = tile[0], tile[1]
    to_a, to_b, to_core, up_0, down_0, up_1, down_1 = routes(n_row, n_col)
    send = lambda v, route: lax.ppermute(v, ("row", "col"), route)

    from_next = [((i + 1) % n_col, i) for i in range(n_col)]
    behind = lax.ppermute(tile, "col", [pair for pair in from_next if not last(pair[1])])
    got_a = send(ga, to_a)
    got_b = send(gb, to_b)
    got_core = send(gb, to_core)
    got_a, got_b, got_core = lax.optimization_barrier((got_a, got_b, got_core))
    a, b, wrap, cross = pick(flags, tile, ga, gb, got_a, got_b, got_core)
    wrap = lax.ppermute(wrap, "col", [pair for pair in from_next if last(pair[1])])
    cross = lax.ppermute(cross, "col", [(0, n_z), (n_z, 0)])
    up = send(a, up_0)
    down = send(b, down_0)
    up, down, cross = lax.optimization_barrier((up, down, cross))
    c, d = turn(flags, a, b, up, down)
    up_2 = send(c, up_0 + up_1)
    down_2 = send(d, down_0 + down_1)
    cross = lax.ppermute(cross, "col", [(0, n_z - 1), (n_z, n_col - 1)])
    up_2, down_2, behind, wrap, cross = lax.optimization_barrier(
        (up_2, down_2, behind, wrap, cross)
    )
    mine, behind = join(flags, wrap, cross, behind, a, b, up, up_2, up_2, down_2, down_2, down)
    other = lax.ppermute(mine, "row", [(i, i ^ 1) for i in range(n_row)])
    return multiply(flags, om, tile, behind, mine, other, slots)


def solution(mesh):
    step = functools.partial(local, n_row=mesh.shape["row"], n_col=mesh.shape["col"])
    return jax.shard_map(
        step,
        mesh=mesh,
        in_specs=(P("col", "row", None), P("col", "row"), P("col", "row")),
        out_specs=P("col", "row", None),
        check_vma=False,
    )
```

```python
import functools

import jax
import jax.numpy as jnp
from jax import lax
from jax.experimental import pallas as pl
from jax.experimental.pallas import tpu as pltpu
from jax.sharding import PartitionSpec as P

HALF = 2
SUB = 32
LANES = 128
AHEAD = 6
FIRST, WHICH, ROLE, HEAD, LAST, SECTION = range(6)
CROSS = 35
LEFT = 32
VMEM = pl.BlockSpec(memory_space=pltpu.VMEM)
SMEM = pl.BlockSpec(memory_space=pltpu.SMEM)


def prep_kernel(flags, table, tile, g, om_ref, flat, index):
    rows, slots, size = tile.shape
    tiles = size // LANES
    first = flags[FIRST]
    lane = lax.broadcasted_iota(jnp.int32, (1, LANES), 1)
    g[:, rows:] = jnp.zeros((2, g.shape[1] - rows) + g.shape[2:], g.dtype)
    index[...] = jnp.zeros(index.shape, index.dtype)

    def row(i, _):
        buf = lax.rem(i, 2)
        count = table[slots, i]
        used = [jnp.int32(0), jnp.int32(0)]
        at = [jnp.int32(0)] * (2 * HALF)
        col = [jnp.int32(-1)] * (2 * HALF)
        out_row = jnp.full((1, LANES), -1, jnp.int32)
        for j in range(slots):
            c = table[j, i]
            live = j < count
            second = (c >= rows).astype(jnp.int32)
            side = jnp.where(second == first, 0, 1)
            for x in range(2):
                here = live & (side == x)
                for k in range(HALF):
                    take = here & (used[x] == k)
                    at[x * HALF + k] = jnp.where(take, j, at[x * HALF + k])
                    col[x * HALF + k] = jnp.where(take, c, col[x * HALF + k])
                used[x] = used[x] + here.astype(jnp.int32)
            out_row = jnp.where(
                (lane < 16) & ((lane & 3) == j), jnp.where(live, c + 1, -1), out_row
            )
        om_ref[pl.ds(i, 1), :] = out_row.astype(jnp.float32)
        idx_row = jnp.zeros((1, LANES), jnp.int32)
        for r in range(2 * HALF):
            inner = jnp.where(col[r] >= rows, col[r] - rows, col[r])
            idx_row = jnp.where((lane < 16) & ((lane >> 2) == r), col[r] + 1, idx_row)
            idx_row = jnp.where(lane == LEFT + r, jnp.where(col[r] < 0, 255, inner), idx_row)
        index[pl.ds(i, 1), :] = idx_row.astype(jnp.float32)
        v = tile[i].astype(jnp.float32)
        for t in range(tiles):
            flat[buf, pl.ds(slots * t, slots), :] = v[:, t * LANES : (t + 1) * LANES]
        for r in range(2 * HALF):
            x = flat[buf, pl.ds(at[r], SUB, stride=slots), :].astype(g.dtype)
            g[r // HALF, i, r % HALF] = x
        return 0

    lax.fori_loop(0, rows, row, 0)
    packed = index[...].astype(g.dtype)
    for x in range(2):
        for k in range(HALF):
            g[x, rows, k] = packed[k * SUB : (k + 1) * SUB]


def prep(flags, table, tile):
    rows, slots, size = tile.shape
    return pl.pallas_call(
        prep_kernel,
        out_shape=(
            jax.ShapeDtypeStruct((2, rows + 2, HALF, SUB, LANES), tile.dtype),
            jax.ShapeDtypeStruct((rows, LANES), jnp.float32),
        ),
        in_specs=[SMEM, SMEM, VMEM],
        out_specs=(VMEM, VMEM),
        scratch_shapes=[
            pltpu.VMEM((2, slots * size // LANES, LANES), jnp.float32),
            pltpu.VMEM((HALF * SUB, LANES), jnp.float32),
        ],
        compiler_params=pltpu.CompilerParams(vmem_limit_bytes=12 << 20),
        name="prep",
    )(flags, table, tile)


def pick_kernel(flags, *refs):
    *sources, tile, a, b, whole, cross = refs
    mid = a.shape[0]
    for n, src in enumerate(sources):

        @pl.when(flags[WHICH] == n)
        def _(src=src):
            a[...] = src[:mid]
            b[...] = src[mid:]

    @pl.when(flags[HEAD] != 0)
    def _():
        rest = tile.shape[1] - CROSS
        whole[: tile.shape[1]] = tile[0]
        whole[tile.shape[1] :] = tile[1, :rest]
        cross[...] = tile[1, rest:]


def pick(flags, tile, *sources):
    shape = tile.shape[1:]
    piece = lambda n: jax.ShapeDtypeStruct((n,) + shape[1:], tile.dtype)
    return pl.pallas_call(
        pick_kernel,
        out_shape=(
            piece(shape[0] // 2),
            piece(shape[0] // 2),
            piece(2 * shape[0] - CROSS),
            piece(CROSS),
        ),
        in_specs=[SMEM] + [VMEM] * (len(sources) + 1),
        out_specs=(VMEM,) * 4,
        compiler_params=pltpu.CompilerParams(vmem_limit_bytes=4 << 20),
        name="pick",
    )(flags, *sources, tile)


def turn_kernel(flags, a, b, up, down, c, d):
    role = flags[ROLE]

    @pl.when(role == 0)
    def _():
        c[...] = b[...]
        d[...] = a[...]

    @pl.when(role == 1)
    def _():
        c[...] = up[...]

    @pl.when(role == 3)
    def _():
        d[...] = down[...]


def turn(flags, *pieces):
    piece = jax.ShapeDtypeStruct(pieces[0].shape, pieces[0].dtype)
    return pl.pallas_call(
        turn_kernel,
        out_shape=(piece, piece),
        in_specs=[SMEM] + [VMEM] * len(pieces),
        out_specs=(VMEM, VMEM),
        compiler_params=pltpu.CompilerParams(vmem_limit_bytes=4 << 20),
        name="turn",
    )(flags, *pieces)


def join_kernel(flags, *refs):
    *pieces, wrap, cross, behind, out, right = refs
    mid = pieces[0].shape[0]
    for role in range(4):

        @pl.when(flags[ROLE] == role)
        def _(role=role):
            out[:mid] = pieces[2 * role][...]
            out[mid:] = pieces[2 * role + 1][...]

    @pl.when(flags[LAST] != 0)
    def _():
        rest = right.shape[1] - CROSS
        right[0] = wrap[: right.shape[1]]
        right[1, :rest] = wrap[right.shape[1] :]
        right[1, rest:] = cross[...]


def join(flags, wrap, cross, behind, *pieces):
    shape = pieces[0].shape
    return pl.pallas_call(
        join_kernel,
        out_shape=(
            jax.ShapeDtypeStruct((2 * shape[0],) + shape[1:], pieces[0].dtype),
            jax.ShapeDtypeStruct(behind.shape, behind.dtype),
        ),
        in_specs=[SMEM] + [VMEM] * (len(pieces) + 3),
        out_specs=(VMEM, VMEM),
        input_output_aliases={len(pieces) + 3: 1},
        compiler_params=pltpu.CompilerParams(vmem_limit_bytes=4 << 20),
        name="join",
    )(flags, *pieces, wrap, cross, behind)


def multiply_kernel(phase, flags, om_ref, own, behind, left, *refs):
    if phase == 0:
        acc, found_ref, tsm, todo, table, wide, tsem = refs
    else:
        before, _, out_ref, acc, tsm, todo, table, wide, tsem = refs
    rows = om_ref.shape[0]
    slots = 2 * HALF
    s = flags[SECTION] if phase == 0 else 1 - flags[SECTION]
    lane = lax.broadcasted_iota(jnp.int32, (rows, LANES), 1)
    low = lax.broadcasted_iota(jnp.int32, (2 * SUB, LANES), 1) < LANES // 2
    weight = jnp.zeros((rows, LANES), jnp.float32)
    for r in range(2 * HALF):
        weight = jnp.where((lane >> 2) == r, ((lane & 3) + 1).astype(jnp.float32) * 8.0**r, weight)
    weight = jnp.where(lane < 16, weight, 0.0)
    found = jnp.zeros((rows, LANES), jnp.float32)
    total = jnp.zeros((rows, 1), jnp.float32)
    om = om_ref[...]
    index = lambda ref: jnp.concatenate([ref(k) for k in range(HALF)], 0).astype(jnp.float32)
    rm = jnp.where(s == 0, index(lambda k: own[0, rows, k]), index(lambda k: behind[0, rows, k]))
    rm = rm.astype(own.dtype)
    lm = index(lambda k: left[rows, k])[:rows]
    for k in range(HALF):
        e = jnp.sum(jnp.where(lane == LEFT + HALF * s + k, lm, 0.0), axis=1, keepdims=True)
        pick = (lane[:, : HALF * SUB].astype(jnp.float32) == e).astype(rm.dtype)
        got = jnp.dot(pick, rm, preferred_element_type=jnp.float32)
        code = jnp.sum(jnp.where(got == om, weight, 0.0), axis=1, keepdims=True)
        found = jnp.where(lane == k, code, found)
        found = jnp.where(lane == 8 + k, e, found)
        total = total + code
    found = jnp.where(lane == 4, total, found)
    if phase == 0:
        found_ref[...] = found
    else:
        was = jnp.sum(jnp.where(lane == 4, before[...], 0.0), axis=1, keepdims=True)
        found = jnp.where(lane == 5, was, jnp.where(lane == 6, was + total, found))
    table[...] = found.astype(jnp.int32)
    put = pltpu.make_async_copy(table, tsm, tsem)
    put.start()
    put.wait()

    def scan(i, n):
        def some(n):
            def clear():
                acc[i] = jnp.zeros(acc.shape[1:], acc.dtype)

            if phase == 0:
                clear()
            else:
                pl.when(tsm[i, 5] == 0)(clear)
            for k in range(HALF):
                code = tsm[i, k]
                base = (i << 16) | (tsm[i, 8 + k] << 8) | (k << 5)
                for r in range(2 * HALF):
                    j = lax.shift_right_logical(code, 3 * r) & 7
                    todo[n] = base | (r << 3) | (j - 1)
                    n = n + (j != 0).astype(jnp.int32)
            return n

        return lax.cond(tsm[i, 4] != 0, some, lambda n: n, n)

    n_todo = lax.fori_loop(0, rows, scan, jnp.int32(0), unroll=4)
    for u in range(AHEAD):
        todo[n_todo + u] = rows << 16
    acc[rows] = jnp.zeros(acc.shape[1:], acc.dtype)

    def pairs(m, _):
        items = []
        for u in range(AHEAD):
            w = todo[m * AHEAD + u]
            i = lax.shift_right_logical(w, 16)
            e = lax.shift_right_logical(w, 8) & 63
            k = lax.shift_right_logical(w, 5) & 1
            x = lax.shift_right_logical(w, 4) & 1
            h = lax.shift_right_logical(w, 3) & 1
            b = jnp.where(s == 0, own[x, e, h].astype(jnp.float32), behind[x, e, h].astype(jnp.float32))
            wide[u, pl.ds(0, SUB, stride=2), :] = b
            wide[u, pl.ds(1, SUB, stride=2), :] = pltpu.roll(b, LANES // 2, 1)
            items.append((i, w & 3, left[i, k]))
        sums = []
        for u, (_, _, a) in enumerate(items):
            v = wide[u]
            diag = jnp.concatenate(
                [jnp.where(low, v, 0.0), jnp.where(low, 0.0, pltpu.roll(v, LANES // 2, 1))], 0
            ).astype(left.dtype)
            sums.append(jnp.dot(a, diag, preferred_element_type=jnp.float32))
        for (i, j, _), got in zip(items, sums):
            at = pl.ds(j, SUB, stride=slots)
            acc[i, at, :] = acc[i, at, :] + got
        return 0

    lax.fori_loop(0, (n_todo + AHEAD - 1) // AHEAD, pairs, 0)

    if phase == 0:
        return

    def finish(i, _):
        @pl.when(tsm[i, 6] == 0)
        def _():
            out_ref[i] = jnp.zeros(out_ref.shape[1:], out_ref.dtype)

        @pl.when(tsm[i, 6] != 0)
        def _():
            for t in range(out_ref.shape[2] // LANES):
                out_ref[i, :, t * LANES : (t + 1) * LANES] = acc[
                    i, pl.ds(slots * t, slots), :
                ].astype(out_ref.dtype)

        return 0

    lax.fori_loop(0, rows, finish, 0, unroll=4)


def multiply(phase, flags, om, own, behind, left, *sums):
    rows = om.shape[0]
    slots = 2 * HALF
    size = SUB * LANES
    acc = jax.ShapeDtypeStruct((rows + 1, slots * size // LANES, LANES), jnp.float32)
    out = (acc, jax.ShapeDtypeStruct(om.shape, om.dtype))
    if phase:
        out = (jax.ShapeDtypeStruct((rows, slots, size), own.dtype), acc)
    return pl.pallas_call(
        functools.partial(multiply_kernel, phase),
        out_shape=out,
        in_specs=[SMEM] + [VMEM] * (4 + len(sums)),
        out_specs=(VMEM, VMEM),
        scratch_shapes=[
            pltpu.SMEM((rows, LANES), jnp.int32),
            pltpu.SMEM((rows * slots * HALF + 2 * AHEAD,), jnp.int32),
            pltpu.VMEM((rows, LANES), jnp.int32),
            pltpu.VMEM((AHEAD, 2 * SUB, LANES), jnp.float32),
            pltpu.SemaphoreType.DMA,
        ],
        input_output_aliases={6: 1} if phase else {},
        compiler_params=pltpu.CompilerParams(vmem_limit_bytes=12 << 20),
        cost_estimate=pl.CostEstimate(flops=10**9, bytes_accessed=4 << 20, transcendentals=0),
        name="multiply%d" % phase,
    )(flags, om, own, behind, left, *sums)


def routes(n_row, n_col):
    to_a, to_b, to_core = [], [], []
    up, down, up_on, down_on = [], [], [], []
    for c in range(n_col):
        owner_a = c // 2
        owner_b = owner_a if c % 2 == 0 else (owner_a + 1) % n_row
        tree_b = owner_b ^ 1 if c % 2 == 0 else owner_b
        rank = lambda q: q * n_col + c
        to_a.append((rank(owner_a), rank(owner_a ^ 8)))
        to_b.append((rank(owner_b), rank(tree_b ^ 8)))
        if owner_b != tree_b:
            to_core.append((rank(owner_b), rank(tree_b)))
        for root in (owner_a, tree_b):
            for x in (0, 8):
                y = (root >> 1) & 3
                at = lambda d: rank((root & 8) ^ x | ((y + d) & 3) << 1 | root & 1)
                up.append((at(0), at(1)))
                down.append((at(0), at(3)))
                up_on.append((at(1), at(2)))
                down_on.append((at(3), at(2)))
    return to_a, to_b, to_core, up, down, up_on, down_on


def local(blocks, columns, counts, n_row, n_col):
    p = lax.axis_index("col")
    q = lax.axis_index("row")
    k = p // 2
    even = p % 2 == 0
    root_a = k
    root_b = jnp.where(even, k ^ 1, (k + 1) % n_row)
    in_a = (q & 1) == (root_a & 1)
    root = jnp.where(in_a, root_a, root_b)
    role = (((q >> 1) & 3) - ((root >> 1) & 3)) & 3
    which = jnp.where(
        in_a,
        jnp.where(q == root_a, 0, 2),
        jnp.where(q == root_b, jnp.where(even, 4, 1), 3),
    )
    which = jnp.where(role == 0, which, -1)
    n_z = n_col // 2
    last = lambda i: (i + 1) % n_z == 0
    flags = [p % 2, which, role, p % n_z == 0, last(p), jnp.where(in_a, 0, 1)]
    flags = jnp.stack([v.astype(jnp.int32) for v in flags])

    table = jnp.concatenate([columns.T, counts.T], 0)
    tile, om = prep(flags, table, blocks)
    ga, gb = tile[0], tile[1]
    to_a, to_b, to_core, up_0, down_0, up_1, down_1 = routes(n_row, n_col)
    send = lambda v, route: lax.ppermute(v, ("row", "col"), route)

    from_next = [((i + 1) % n_col, i) for i in range(n_col)]
    behind = lax.ppermute(tile, "col", [pair for pair in from_next if not last(pair[1])])
    got_a = send(ga, to_a)
    got_b = send(gb, to_b)
    got_core = send(gb, to_core)
    got_a, got_b, got_core = lax.optimization_barrier((got_a, got_b, got_core))
    a, b, wrap, cross = pick(flags, tile, ga, gb, got_a, got_b, got_core)
    wrap = lax.ppermute(wrap, "col", [pair for pair in from_next if last(pair[1])])
    cross = lax.ppermute(cross, "col", [(0, n_z), (n_z, 0)])
    up = send(a, up_0)
    down = send(b, down_0)
    up, down, cross = lax.optimization_barrier((up, down, cross))
    c, d = turn(flags, a, b, up, down)
    up_2 = send(c, up_0 + up_1)
    down_2 = send(d, down_0 + down_1)
    cross = lax.ppermute(cross, "col", [(0, n_z - 1), (n_z, n_col - 1)])
    up_2, down_2, behind, wrap, cross = lax.optimization_barrier(
        (up_2, down_2, behind, wrap, cross)
    )
    mine, behind = join(flags, wrap, cross, behind, a, b, up, up_2, up_2, down_2, down_2, down)
    other = lax.ppermute(mine, "row", [(i, i ^ 1) for i in range(n_row)])
    sums, found = multiply(0, flags, om, tile, behind, mine)
    return multiply(1, flags, om, tile, behind, other, found, sums)[0]


def solution(mesh):
    step = functools.partial(local, n_row=mesh.shape["row"], n_col=mesh.shape["col"])
    return jax.shard_map(
        step,
        mesh=mesh,
        in_specs=(P("col", "row", None), P("col", "row"), P("col", "row")),
        out_specs=P("col", "row", None),
        check_vma=False,
    )
```

```python
import functools

import jax
import jax.numpy as jnp
from jax import lax
from jax.experimental import pallas as pl
from jax.experimental.pallas import tpu as pltpu
from jax.sharding import PartitionSpec as P

HALF = 2
SUB = 32
LANES = 128
AHEAD = 6
FIRST, WHICH, ROLE, HEAD, LAST, SECTION = range(6)
CROSS = 35
LEFT = 32
VMEM = pl.BlockSpec(memory_space=pltpu.VMEM)
SMEM = pl.BlockSpec(memory_space=pltpu.SMEM)


def prep_kernel(flags, table, tile, g, om_ref, flat, index):
    rows, slots, size = tile.shape
    tiles = size // LANES
    first = flags[FIRST]
    lane = lax.broadcasted_iota(jnp.int32, (1, LANES), 1)
    g[:, rows:] = jnp.zeros((2, g.shape[1] - rows) + g.shape[2:], g.dtype)
    index[...] = jnp.zeros(index.shape, index.dtype)

    def row(i, _):
        buf = lax.rem(i, 2)
        count = table[slots, i]
        used = [jnp.int32(0), jnp.int32(0)]
        at = [jnp.int32(0)] * (2 * HALF)
        col = [jnp.int32(-1)] * (2 * HALF)
        out_row = jnp.full((1, LANES), -1, jnp.int32)
        for j in range(slots):
            c = table[j, i]
            live = j < count
            second = (c >= rows).astype(jnp.int32)
            side = jnp.where(second == first, 0, 1)
            for x in range(2):
                here = live & (side == x)
                for k in range(HALF):
                    take = here & (used[x] == k)
                    at[x * HALF + k] = jnp.where(take, j, at[x * HALF + k])
                    col[x * HALF + k] = jnp.where(take, c, col[x * HALF + k])
                used[x] = used[x] + here.astype(jnp.int32)
            out_row = jnp.where(
                (lane < 16) & ((lane & 3) == j), jnp.where(live, c + 1, -1), out_row
            )
        om_ref[pl.ds(i, 1), :] = out_row.astype(jnp.float32)
        idx_row = jnp.zeros((1, LANES), jnp.int32)
        for r in range(2 * HALF):
            inner = jnp.where(col[r] >= rows, col[r] - rows, col[r])
            idx_row = jnp.where((lane < 16) & ((lane >> 2) == r), col[r] + 1, idx_row)
            idx_row = jnp.where(lane == LEFT + r, jnp.where(col[r] < 0, 255, inner), idx_row)
        index[pl.ds(i, 1), :] = idx_row.astype(jnp.float32)
        v = tile[i].astype(jnp.float32)
        for t in range(tiles):
            flat[buf, pl.ds(slots * t, slots), :] = v[:, t * LANES : (t + 1) * LANES]
        for r in range(2 * HALF):
            x = flat[buf, pl.ds(at[r], SUB, stride=slots), :].astype(g.dtype)
            g[r // HALF, i, r % HALF] = x
        return 0

    lax.fori_loop(0, rows, row, 0)
    packed = index[...].astype(g.dtype)
    for x in range(2):
        for k in range(HALF):
            g[x, rows, k] = packed[k * SUB : (k + 1) * SUB]


def prep(flags, table, tile):
    rows, slots, size = tile.shape
    return pl.pallas_call(
        prep_kernel,
        out_shape=(
            jax.ShapeDtypeStruct((2, rows + 2, HALF, SUB, LANES), tile.dtype),
            jax.ShapeDtypeStruct((rows, LANES), jnp.float32),
        ),
        in_specs=[SMEM, SMEM, VMEM],
        out_specs=(VMEM, VMEM),
        scratch_shapes=[
            pltpu.VMEM((2, slots * size // LANES, LANES), jnp.float32),
            pltpu.VMEM((HALF * SUB, LANES), jnp.float32),
        ],
        compiler_params=pltpu.CompilerParams(vmem_limit_bytes=12 << 20),
        name="prep",
    )(flags, table, tile)


def pick_kernel(flags, *refs):
    *sources, tile, a, b, whole, cross = refs
    mid = a.shape[0]
    for n, src in enumerate(sources):

        @pl.when(flags[WHICH] == n)
        def _(src=src):
            a[...] = src[:mid]
            b[...] = src[mid:]

    @pl.when(flags[HEAD] != 0)
    def _():
        rest = tile.shape[1] - CROSS
        whole[: tile.shape[1]] = tile[0]
        whole[tile.shape[1] :] = tile[1, :rest]
        cross[...] = tile[1, rest:]


def pick(flags, tile, *sources):
    shape = tile.shape[1:]
    piece = lambda n: jax.ShapeDtypeStruct((n,) + shape[1:], tile.dtype)
    return pl.pallas_call(
        pick_kernel,
        out_shape=(
            piece(shape[0] // 2),
            piece(shape[0] // 2),
            piece(2 * shape[0] - CROSS),
            piece(CROSS),
        ),
        in_specs=[SMEM] + [VMEM] * (len(sources) + 1),
        out_specs=(VMEM,) * 4,
        compiler_params=pltpu.CompilerParams(vmem_limit_bytes=4 << 20),
        name="pick",
    )(flags, *sources, tile)


def turn_kernel(flags, a, b, up, down, c, d):
    role = flags[ROLE]

    @pl.when(role == 0)
    def _():
        c[...] = b[...]
        d[...] = a[...]

    @pl.when(role == 1)
    def _():
        c[...] = up[...]

    @pl.when(role == 3)
    def _():
        d[...] = down[...]


def turn(flags, *pieces):
    piece = jax.ShapeDtypeStruct(pieces[0].shape, pieces[0].dtype)
    return pl.pallas_call(
        turn_kernel,
        out_shape=(piece, piece),
        in_specs=[SMEM] + [VMEM] * len(pieces),
        out_specs=(VMEM, VMEM),
        compiler_params=pltpu.CompilerParams(vmem_limit_bytes=4 << 20),
        name="turn",
    )(flags, *pieces)


def join_kernel(flags, *refs):
    *pieces, wrap, cross, behind, out, right = refs
    mid = pieces[0].shape[0]
    for role in range(4):

        @pl.when(flags[ROLE] == role)
        def _(role=role):
            out[:mid] = pieces[2 * role][...]
            out[mid:] = pieces[2 * role + 1][...]

    @pl.when(flags[LAST] != 0)
    def _():
        rest = right.shape[1] - CROSS
        right[0] = wrap[: right.shape[1]]
        right[1, :rest] = wrap[right.shape[1] :]
        right[1, rest:] = cross[...]


def join(flags, wrap, cross, behind, *pieces):
    shape = pieces[0].shape
    return pl.pallas_call(
        join_kernel,
        out_shape=(
            jax.ShapeDtypeStruct((2 * shape[0],) + shape[1:], pieces[0].dtype),
            jax.ShapeDtypeStruct(behind.shape, behind.dtype),
        ),
        in_specs=[SMEM] + [VMEM] * (len(pieces) + 3),
        out_specs=(VMEM, VMEM),
        input_output_aliases={len(pieces) + 3: 1},
        compiler_params=pltpu.CompilerParams(vmem_limit_bytes=4 << 20),
        name="join",
    )(flags, *pieces, wrap, cross, behind)


def multiply_kernel(phase, flags, om_ref, own, behind, left, *refs):
    if phase == 0:
        acc, found_ref, tsm, todo, table, wide, tsem = refs
    else:
        before, _, out_ref, acc, tsm, todo, table, wide, tsem = refs
    rows = om_ref.shape[0]
    slots = 2 * HALF
    s = flags[SECTION] if phase == 0 else 1 - flags[SECTION]
    lane = lax.broadcasted_iota(jnp.int32, (rows, LANES), 1)
    low = lax.broadcasted_iota(jnp.int32, (2 * SUB, LANES), 1) < LANES // 2
    weight = jnp.zeros((rows, LANES), jnp.float32)
    for r in range(2 * HALF):
        weight = jnp.where((lane >> 2) == r, ((lane & 3) + 1).astype(jnp.float32) * 8.0**r, weight)
    weight = jnp.where(lane < 16, weight, 0.0)
    found = jnp.zeros((rows, LANES), jnp.float32)
    total = jnp.zeros((rows, 1), jnp.float32)
    om = om_ref[...]
    index = lambda ref: jnp.concatenate([ref(k) for k in range(HALF)], 0).astype(jnp.float32)
    rm = jnp.where(s == 0, index(lambda k: own[0, rows, k]), index(lambda k: behind[0, rows, k]))
    rm = rm.astype(own.dtype)
    lm = index(lambda k: left[rows, k])[:rows]
    for k in range(HALF):
        e = jnp.sum(jnp.where(lane == LEFT + HALF * s + k, lm, 0.0), axis=1, keepdims=True)
        pick = (lane[:, : HALF * SUB].astype(jnp.float32) == e).astype(rm.dtype)
        got = jnp.dot(pick, rm, preferred_element_type=jnp.float32)
        code = jnp.sum(jnp.where(got == om, weight, 0.0), axis=1, keepdims=True)
        found = jnp.where(lane == k, code, found)
        found = jnp.where(lane == 8 + k, e, found)
        total = total + code
    found = jnp.where(lane == 4, total, found)
    if phase == 0:
        found_ref[...] = found
    else:
        was = jnp.sum(jnp.where(lane == 4, before[...], 0.0), axis=1, keepdims=True)
        found = jnp.where(lane == 5, was, jnp.where(lane == 6, was + total, found))
    table[...] = found.astype(jnp.int32)
    put = pltpu.make_async_copy(table, tsm, tsem)
    put.start()
    put.wait()

    def scan(i, n):
        def some(n):
            def clear():
                acc[i] = jnp.zeros(acc.shape[1:], acc.dtype)

            if phase == 0:
                clear()
            else:
                pl.when(tsm[i, 5] == 0)(clear)
            for k in range(HALF):
                code = tsm[i, k]
                base = (i << 16) | (tsm[i, 8 + k] << 8) | (k << 5)
                for r in range(2 * HALF):
                    j = lax.shift_right_logical(code, 3 * r) & 7
                    todo[n] = base | (r << 3) | (j - 1)
                    n = n + (j != 0).astype(jnp.int32)
            return n

        return lax.cond(tsm[i, 4] != 0, some, lambda n: n, n)

    n_todo = lax.fori_loop(0, rows, scan, jnp.int32(0), unroll=4)
    for u in range(AHEAD):
        todo[n_todo + u] = rows << 16
    acc[rows] = jnp.zeros(acc.shape[1:], acc.dtype)

    def pairs(m, _):
        items = []
        for u in range(AHEAD):
            w = todo[m * AHEAD + u]
            i = lax.shift_right_logical(w, 16)
            e = lax.shift_right_logical(w, 8) & 63
            k = lax.shift_right_logical(w, 5) & 1
            x = lax.shift_right_logical(w, 4) & 1
            h = lax.shift_right_logical(w, 3) & 1
            b = jnp.where(s == 0, own[x, e, h].astype(jnp.float32), behind[x, e, h].astype(jnp.float32))
            wide[u, pl.ds(0, SUB, stride=2), :] = b
            wide[u, pl.ds(1, SUB, stride=2), :] = pltpu.roll(b, LANES // 2, 1)
            items.append((i, w & 3, left[i, k]))
        sums = []
        for u, (_, _, a) in enumerate(items):
            v = wide[u]
            diag = jnp.concatenate(
                [jnp.where(low, v, 0.0), jnp.where(low, 0.0, pltpu.roll(v, LANES // 2, 1))], 0
            ).astype(left.dtype)
            sums.append(jnp.dot(a, diag, preferred_element_type=jnp.float32))
        for (i, j, _), got in zip(items, sums):
            at = pl.ds(j, SUB, stride=slots)
            acc[i, at, :] = acc[i, at, :] + got
        return 0

    lax.fori_loop(0, (n_todo + AHEAD - 1) // AHEAD, pairs, 0)

    if phase == 0:
        return

    def finish(i, _):
        @pl.when(tsm[i, 6] == 0)
        def _():
            out_ref[i] = jnp.zeros(out_ref.shape[1:], out_ref.dtype)

        @pl.when(tsm[i, 6] != 0)
        def _():
            for t in range(out_ref.shape[2] // LANES):
                out_ref[i, :, t * LANES : (t + 1) * LANES] = acc[
                    i, pl.ds(slots * t, slots), :
                ].astype(out_ref.dtype)

        return 0

    lax.fori_loop(0, rows, finish, 0, unroll=4)


def multiply(phase, flags, om, own, behind, left, *sums):
    rows = om.shape[0]
    slots = 2 * HALF
    size = SUB * LANES
    acc = jax.ShapeDtypeStruct((rows + 1, slots * size // LANES, LANES), jnp.float32)
    out = (acc, jax.ShapeDtypeStruct(om.shape, om.dtype))
    if phase:
        out = (jax.ShapeDtypeStruct((rows, slots, size), own.dtype), acc)
    return pl.pallas_call(
        functools.partial(multiply_kernel, phase),
        out_shape=out,
        in_specs=[SMEM] + [VMEM] * (4 + len(sums)),
        out_specs=(VMEM, VMEM),
        scratch_shapes=[
            pltpu.SMEM((rows, LANES), jnp.int32),
            pltpu.SMEM((rows * slots * HALF + 2 * AHEAD,), jnp.int32),
            pltpu.VMEM((rows, LANES), jnp.int32),
            pltpu.VMEM((AHEAD, 2 * SUB, LANES), jnp.float32),
            pltpu.SemaphoreType.DMA,
        ],
        input_output_aliases={6: 1} if phase else {},
        compiler_params=pltpu.CompilerParams(vmem_limit_bytes=12 << 20),
        cost_estimate=pl.CostEstimate(flops=10**9, bytes_accessed=4 << 20, transcendentals=0),
        name="multiply%d" % phase,
    )(flags, om, own, behind, left, *sums)


def routes(n_row, n_col):
    to_a, to_b, to_core = [], [], []
    up, down, up_on, down_on = [], [], [], []
    for c in range(n_col):
        owner_a = c // 2
        owner_b = owner_a if c % 2 == 0 else (owner_a + 1) % n_row
        tree_b = owner_b ^ 1 if c % 2 == 0 else owner_b
        rank = lambda q: q * n_col + c
        to_a.append((rank(owner_a), rank(owner_a ^ 8)))
        to_b.append((rank(owner_b), rank(tree_b ^ 8)))
        if owner_b != tree_b:
            to_core.append((rank(owner_b), rank(tree_b)))
        for root in (owner_a, tree_b):
            for x in (0, 8):
                y = (root >> 1) & 3
                at = lambda d: rank((root & 8) ^ x | ((y + d) & 3) << 1 | root & 1)
                up.append((at(0), at(1)))
                down.append((at(0), at(3)))
                up_on.append((at(1), at(2)))
                down_on.append((at(3), at(2)))
    return to_a, to_b, to_core, up, down, up_on, down_on


def local(blocks, columns, counts, n_row, n_col):
    p = lax.axis_index("col")
    q = lax.axis_index("row")
    k = p // 2
    even = p % 2 == 0
    root_a = k
    root_b = jnp.where(even, k ^ 1, (k + 1) % n_row)
    in_a = (q & 1) == (root_a & 1)
    root = jnp.where(in_a, root_a, root_b)
    role = (((q >> 1) & 3) - ((root >> 1) & 3)) & 3
    which = jnp.where(
        in_a,
        jnp.where(q == root_a, 0, 2),
        jnp.where(q == root_b, jnp.where(even, 4, 1), 3),
    )
    which = jnp.where(role == 0, which, -1)
    n_z = n_col // 2
    last = lambda i: (i + 1) % n_z == 0
    flags = [p % 2, which, role, p % n_z == 0, last(p), jnp.where(in_a, 0, 1)]
    flags = jnp.stack([v.astype(jnp.int32) for v in flags])

    table = jnp.concatenate([columns.T, counts.T], 0)
    tile, om = prep(flags, table, blocks)
    ga, gb = tile[0], tile[1]
    to_a, to_b, to_core, up_0, down_0, up_1, down_1 = routes(n_row, n_col)
    send = lambda v, route: lax.ppermute(v, ("row", "col"), route)

    from_next = [((i + 1) % n_col, i) for i in range(n_col)]
    behind = lax.ppermute(tile, "col", [pair for pair in from_next if not last(pair[1])])
    got_a = send(ga, to_a)
    got_b = send(gb, to_b)
    got_core = send(gb, to_core)
    got_a, got_b, got_core = lax.optimization_barrier((got_a, got_b, got_core))
    a, b, wrap, cross = pick(flags, tile, ga, gb, got_a, got_b, got_core)
    wrap = lax.ppermute(wrap, "col", [pair for pair in from_next if last(pair[1])])
    cross = lax.ppermute(cross, "col", [(0, n_z), (n_z, 0)])
    up = send(a, up_0)
    down = send(b, down_0)
    up, down = lax.optimization_barrier((up, down))
    c, d = turn(flags, a, b, up, down)
    up_2 = send(c, up_0 + up_1)
    down_2 = send(d, down_0 + down_1)
    cross = lax.ppermute(cross, "col", [(0, n_z - 1), (n_z, n_col - 1)])
    up_2, down_2, behind, wrap, cross = lax.optimization_barrier(
        (up_2, down_2, behind, wrap, cross)
    )
    mine, behind = join(flags, wrap, cross, behind, a, b, up, up_2, up_2, down_2, down_2, down)
    other = lax.ppermute(mine, "row", [(i, i ^ 1) for i in range(n_row)])
    sums, found = multiply(0, flags, om, tile, behind, mine)
    return multiply(1, flags, om, tile, behind, other, found, sums)[0]


def solution(mesh):
    step = functools.partial(local, n_row=mesh.shape["row"], n_col=mesh.shape["col"])
    return jax.shard_map(
        step,
        mesh=mesh,
        in_specs=(P("col", "row", None), P("col", "row"), P("col", "row")),
        out_specs=P("col", "row", None),
        check_vma=False,
    )
```

```python
import functools

import jax
import jax.numpy as jnp
from jax import lax
from jax.experimental import pallas as pl
from jax.experimental.pallas import tpu as pltpu
from jax.sharding import PartitionSpec as P

HALF = 2
SUB = 32
LANES = 128
AHEAD = 8
FIRST, WHICH, ROLE, HEAD, LAST, SECTION = range(6)
CROSS = 35
LEFT = 32
VMEM = pl.BlockSpec(memory_space=pltpu.VMEM)
SMEM = pl.BlockSpec(memory_space=pltpu.SMEM)


def prep_kernel(flags, table, tile, g, om_ref, flat, index):
    rows, slots, size = tile.shape
    tiles = size // LANES
    first = flags[FIRST]
    lane = lax.broadcasted_iota(jnp.int32, (1, LANES), 1)
    g[:, rows:] = jnp.zeros((2, g.shape[1] - rows) + g.shape[2:], g.dtype)
    index[...] = jnp.zeros(index.shape, index.dtype)

    def row(i, _):
        buf = lax.rem(i, 2)
        count = table[slots, i]
        used = [jnp.int32(0), jnp.int32(0)]
        at = [jnp.int32(0)] * (2 * HALF)
        col = [jnp.int32(-1)] * (2 * HALF)
        out_row = jnp.full((1, LANES), -1, jnp.int32)
        for j in range(slots):
            c = table[j, i]
            live = j < count
            second = (c >= rows).astype(jnp.int32)
            side = jnp.where(second == first, 0, 1)
            for x in range(2):
                here = live & (side == x)
                for k in range(HALF):
                    take = here & (used[x] == k)
                    at[x * HALF + k] = jnp.where(take, j, at[x * HALF + k])
                    col[x * HALF + k] = jnp.where(take, c, col[x * HALF + k])
                used[x] = used[x] + here.astype(jnp.int32)
            out_row = jnp.where(
                (lane < 16) & ((lane & 3) == j), jnp.where(live, c + 1, -1), out_row
            )
        om_ref[pl.ds(i, 1), :] = out_row.astype(jnp.float32)
        idx_row = jnp.zeros((1, LANES), jnp.int32)
        for r in range(2 * HALF):
            inner = jnp.where(col[r] >= rows, col[r] - rows, col[r])
            idx_row = jnp.where((lane < 16) & ((lane >> 2) == r), col[r] + 1, idx_row)
            idx_row = jnp.where(lane == LEFT + r, jnp.where(col[r] < 0, 255, inner), idx_row)
        index[pl.ds(i, 1), :] = idx_row.astype(jnp.float32)
        v = tile[i].astype(jnp.float32)
        for t in range(tiles):
            flat[buf, pl.ds(slots * t, slots), :] = v[:, t * LANES : (t + 1) * LANES]
        for r in range(2 * HALF):
            x = flat[buf, pl.ds(at[r], SUB, stride=slots), :].astype(g.dtype)
            g[r // HALF, i, r % HALF] = x
        return 0

    lax.fori_loop(0, rows, row, 0)
    packed = index[...].astype(g.dtype)
    for x in range(2):
        for k in range(HALF):
            g[x, rows, k] = packed[k * SUB : (k + 1) * SUB]


def prep(flags, table, tile):
    rows, slots, size = tile.shape
    return pl.pallas_call(
        prep_kernel,
        out_shape=(
            jax.ShapeDtypeStruct((2, rows + 2, HALF, SUB, LANES), tile.dtype),
            jax.ShapeDtypeStruct((rows, LANES), jnp.float32),
        ),
        in_specs=[SMEM, SMEM, VMEM],
        out_specs=(VMEM, VMEM),
        scratch_shapes=[
            pltpu.VMEM((2, slots * size // LANES, LANES), jnp.float32),
            pltpu.VMEM((HALF * SUB, LANES), jnp.float32),
        ],
        compiler_params=pltpu.CompilerParams(vmem_limit_bytes=12 << 20),
        name="prep",
    )(flags, table, tile)


def pick_kernel(flags, *refs):
    *sources, tile, a, b, whole, cross = refs
    mid = a.shape[0]
    for n, src in enumerate(sources):

        @pl.when(flags[WHICH] == n)
        def _(src=src):
            a[...] = src[:mid]
            b[...] = src[mid:]

    @pl.when(flags[HEAD] != 0)
    def _():
        rest = tile.shape[1] - CROSS
        whole[: tile.shape[1]] = tile[0]
        whole[tile.shape[1] :] = tile[1, :rest]
        cross[...] = tile[1, rest:]


def pick(flags, tile, *sources):
    shape = tile.shape[1:]
    piece = lambda n: jax.ShapeDtypeStruct((n,) + shape[1:], tile.dtype)
    return pl.pallas_call(
        pick_kernel,
        out_shape=(
            piece(shape[0] // 2),
            piece(shape[0] // 2),
            piece(2 * shape[0] - CROSS),
            piece(CROSS),
        ),
        in_specs=[SMEM] + [VMEM] * (len(sources) + 1),
        out_specs=(VMEM,) * 4,
        compiler_params=pltpu.CompilerParams(vmem_limit_bytes=4 << 20),
        name="pick",
    )(flags, *sources, tile)


def turn_kernel(flags, a, b, up, down, c, d):
    role = flags[ROLE]

    @pl.when(role == 0)
    def _():
        c[...] = b[...]
        d[...] = a[...]

    @pl.when(role == 1)
    def _():
        c[...] = up[...]

    @pl.when(role == 3)
    def _():
        d[...] = down[...]


def turn(flags, *pieces):
    piece = jax.ShapeDtypeStruct(pieces[0].shape, pieces[0].dtype)
    return pl.pallas_call(
        turn_kernel,
        out_shape=(piece, piece),
        in_specs=[SMEM] + [VMEM] * len(pieces),
        out_specs=(VMEM, VMEM),
        compiler_params=pltpu.CompilerParams(vmem_limit_bytes=4 << 20),
        name="turn",
    )(flags, *pieces)


def join_kernel(flags, *refs):
    *pieces, wrap, cross, behind, out, right = refs
    mid = pieces[0].shape[0]
    for role in range(4):

        @pl.when(flags[ROLE] == role)
        def _(role=role):
            out[:mid] = pieces[2 * role][...]
            out[mid:] = pieces[2 * role + 1][...]

    @pl.when(flags[LAST] != 0)
    def _():
        rest = right.shape[1] - CROSS
        right[0] = wrap[: right.shape[1]]
        right[1, :rest] = wrap[right.shape[1] :]
        right[1, rest:] = cross[...]


def join(flags, wrap, cross, behind, *pieces):
    shape = pieces[0].shape
    return pl.pallas_call(
        join_kernel,
        out_shape=(
            jax.ShapeDtypeStruct((2 * shape[0],) + shape[1:], pieces[0].dtype),
            jax.ShapeDtypeStruct(behind.shape, behind.dtype),
        ),
        in_specs=[SMEM] + [VMEM] * (len(pieces) + 3),
        out_specs=(VMEM, VMEM),
        input_output_aliases={len(pieces) + 3: 1},
        compiler_params=pltpu.CompilerParams(vmem_limit_bytes=4 << 20),
        name="join",
    )(flags, *pieces, wrap, cross, behind)


def multiply_kernel(phase, flags, om_ref, own, behind, left, *refs):
    if phase == 0:
        acc, found_ref, tsm, todo, table, wide, tsem = refs
    else:
        before, _, out_ref, acc, tsm, todo, table, wide, tsem = refs
    rows = om_ref.shape[0]
    slots = 2 * HALF
    s = flags[SECTION] if phase == 0 else 1 - flags[SECTION]
    lane = lax.broadcasted_iota(jnp.int32, (rows, LANES), 1)
    low = lax.broadcasted_iota(jnp.int32, (2 * SUB, LANES), 1) < LANES // 2
    weight = jnp.zeros((rows, LANES), jnp.float32)
    for r in range(2 * HALF):
        weight = jnp.where((lane >> 2) == r, ((lane & 3) + 1).astype(jnp.float32) * 8.0**r, weight)
    weight = jnp.where(lane < 16, weight, 0.0)
    found = jnp.zeros((rows, LANES), jnp.float32)
    total = jnp.zeros((rows, 1), jnp.float32)
    om = om_ref[...]
    index = lambda ref: jnp.concatenate([ref(k) for k in range(HALF)], 0).astype(jnp.float32)
    rm = jnp.where(s == 0, index(lambda k: own[0, rows, k]), index(lambda k: behind[0, rows, k]))
    rm = rm.astype(own.dtype)
    lm = index(lambda k: left[rows, k])[:rows]
    for k in range(HALF):
        e = jnp.sum(jnp.where(lane == LEFT + HALF * s + k, lm, 0.0), axis=1, keepdims=True)
        pick = (lane[:, : HALF * SUB].astype(jnp.float32) == e).astype(rm.dtype)
        got = jnp.dot(pick, rm, preferred_element_type=jnp.float32)
        code = jnp.sum(jnp.where(got == om, weight, 0.0), axis=1, keepdims=True)
        found = jnp.where(lane == k, code, found)
        found = jnp.where(lane == 8 + k, e, found)
        total = total + code
    found = jnp.where(lane == 4, total, found)
    if phase == 0:
        found_ref[...] = found
    else:
        was = jnp.sum(jnp.where(lane == 4, before[...], 0.0), axis=1, keepdims=True)
        found = jnp.where(lane == 5, was, jnp.where(lane == 6, was + total, found))
    table[...] = found.astype(jnp.int32)
    put = pltpu.make_async_copy(table, tsm, tsem)
    put.start()
    put.wait()

    def scan(i, n):
        def some(n):
            def clear():
                acc[i] = jnp.zeros(acc.shape[1:], acc.dtype)

            if phase == 0:
                clear()
            else:
                pl.when(tsm[i, 5] == 0)(clear)
            for k in range(HALF):
                code = tsm[i, k]
                base = (i << 16) | (tsm[i, 8 + k] << 8) | (k << 5)
                for r in range(2 * HALF):
                    j = lax.shift_right_logical(code, 3 * r) & 7
                    todo[n] = base | (r << 3) | (j - 1)
                    n = n + (j != 0).astype(jnp.int32)
            return n

        return lax.cond(tsm[i, 4] != 0, some, lambda n: n, n)

    n_todo = lax.fori_loop(0, rows, scan, jnp.int32(0), unroll=4)
    for u in range(AHEAD):
        todo[n_todo + u] = rows << 16
    acc[rows] = jnp.zeros(acc.shape[1:], acc.dtype)

    def pairs(m, _):
        items = []
        for u in range(AHEAD):
            w = todo[m * AHEAD + u]
            i = lax.shift_right_logical(w, 16)
            e = lax.shift_right_logical(w, 8) & 63
            k = lax.shift_right_logical(w, 5) & 1
            x = lax.shift_right_logical(w, 4) & 1
            h = lax.shift_right_logical(w, 3) & 1
            b = jnp.where(s == 0, own[x, e, h].astype(jnp.float32), behind[x, e, h].astype(jnp.float32))
            wide[u, pl.ds(0, SUB, stride=2), :] = b
            wide[u, pl.ds(1, SUB, stride=2), :] = pltpu.roll(b, LANES // 2, 1)
            items.append((i, w & 3, left[i, k]))
        sums = []
        for u, (_, _, a) in enumerate(items):
            v = wide[u]
            diag = jnp.concatenate(
                [jnp.where(low, v, 0.0), jnp.where(low, 0.0, pltpu.roll(v, LANES // 2, 1))], 0
            ).astype(left.dtype)
            sums.append(jnp.dot(a, diag, preferred_element_type=jnp.float32))
        for (i, j, _), got in zip(items, sums):
            at = pl.ds(j, SUB, stride=slots)
            acc[i, at, :] = acc[i, at, :] + got
        return 0

    lax.fori_loop(0, (n_todo + AHEAD - 1) // AHEAD, pairs, 0)

    if phase == 0:
        return

    def finish(i, _):
        @pl.when(tsm[i, 6] == 0)
        def _():
            out_ref[i] = jnp.zeros(out_ref.shape[1:], out_ref.dtype)

        @pl.when(tsm[i, 6] != 0)
        def _():
            for t in range(out_ref.shape[2] // LANES):
                out_ref[i, :, t * LANES : (t + 1) * LANES] = acc[
                    i, pl.ds(slots * t, slots), :
                ].astype(out_ref.dtype)

        return 0

    lax.fori_loop(0, rows, finish, 0, unroll=4)


def multiply(phase, flags, om, own, behind, left, *sums):
    rows = om.shape[0]
    slots = 2 * HALF
    size = SUB * LANES
    acc = jax.ShapeDtypeStruct((rows + 1, slots * size // LANES, LANES), jnp.float32)
    out = (acc, jax.ShapeDtypeStruct(om.shape, om.dtype))
    if phase:
        out = (jax.ShapeDtypeStruct((rows, slots, size), own.dtype), acc)
    return pl.pallas_call(
        functools.partial(multiply_kernel, phase),
        out_shape=out,
        in_specs=[SMEM] + [VMEM] * (4 + len(sums)),
        out_specs=(VMEM, VMEM),
        scratch_shapes=[
            pltpu.SMEM((rows, LANES), jnp.int32),
            pltpu.SMEM((rows * slots * HALF + 2 * AHEAD,), jnp.int32),
            pltpu.VMEM((rows, LANES), jnp.int32),
            pltpu.VMEM((AHEAD, 2 * SUB, LANES), jnp.float32),
            pltpu.SemaphoreType.DMA,
        ],
        input_output_aliases={6: 1} if phase else {},
        compiler_params=pltpu.CompilerParams(vmem_limit_bytes=12 << 20),
        cost_estimate=pl.CostEstimate(flops=10**9, bytes_accessed=4 << 20, transcendentals=0),
        name="multiply%d" % phase,
    )(flags, om, own, behind, left, *sums)


def routes(n_row, n_col):
    to_a, to_b, to_core = [], [], []
    up, down, up_on, down_on = [], [], [], []
    for c in range(n_col):
        owner_a = c // 2
        owner_b = owner_a if c % 2 == 0 else (owner_a + 1) % n_row
        tree_b = owner_b ^ 1 if c % 2 == 0 else owner_b
        rank = lambda q: q * n_col + c
        to_a.append((rank(owner_a), rank(owner_a ^ 8)))
        to_b.append((rank(owner_b), rank(tree_b ^ 8)))
        if owner_b != tree_b:
            to_core.append((rank(owner_b), rank(tree_b)))
        for root in (owner_a, tree_b):
            for x in (0, 8):
                y = (root >> 1) & 3
                at = lambda d: rank((root & 8) ^ x | ((y + d) & 3) << 1 | root & 1)
                up.append((at(0), at(1)))
                down.append((at(0), at(3)))
                up_on.append((at(1), at(2)))
                down_on.append((at(3), at(2)))
    return to_a, to_b, to_core, up, down, up_on, down_on


def local(blocks, columns, counts, n_row, n_col):
    p = lax.axis_index("col")
    q = lax.axis_index("row")
    k = p // 2
    even = p % 2 == 0
    root_a = k
    root_b = jnp.where(even, k ^ 1, (k + 1) % n_row)
    in_a = (q & 1) == (root_a & 1)
    root = jnp.where(in_a, root_a, root_b)
    role = (((q >> 1) & 3) - ((root >> 1) & 3)) & 3
    which = jnp.where(
        in_a,
        jnp.where(q == root_a, 0, 2),
        jnp.where(q == root_b, jnp.where(even, 4, 1), 3),
    )
    which = jnp.where(role == 0, which, -1)
    n_z = n_col // 2
    last = lambda i: (i + 1) % n_z == 0
    flags = [p % 2, which, role, p % n_z == 0, last(p), jnp.where(in_a, 0, 1)]
    flags = jnp.stack([v.astype(jnp.int32) for v in flags])

    table = jnp.concatenate([columns.T, counts.T], 0)
    tile, om = prep(flags, table, blocks)
    ga, gb = tile[0], tile[1]
    to_a, to_b, to_core, up_0, down_0, up_1, down_1 = routes(n_row, n_col)
    send = lambda v, route: lax.ppermute(v, ("row", "col"), route)

    from_next = [((i + 1) % n_col, i) for i in range(n_col)]
    behind = lax.ppermute(tile, "col", [pair for pair in from_next if not last(pair[1])])
    got_a = send(ga, to_a)
    got_b = send(gb, to_b)
    got_core = send(gb, to_core)
    got_a, got_b, got_core = lax.optimization_barrier((got_a, got_b, got_core))
    a, b, wrap, cross = pick(flags, tile, ga, gb, got_a, got_b, got_core)
    wrap = lax.ppermute(wrap, "col", [pair for pair in from_next if last(pair[1])])
    cross = lax.ppermute(cross, "col", [(0, n_z), (n_z, 0)])
    up = send(a, up_0)
    down = send(b, down_0)
    up, down = lax.optimization_barrier((up, down))
    c, d = turn(flags, a, b, up, down)
    up_2 = send(c, up_0 + up_1)
    down_2 = send(d, down_0 + down_1)
    cross = lax.ppermute(cross, "col", [(0, n_z - 1), (n_z, n_col - 1)])
    up_2, down_2, behind, wrap, cross = lax.optimization_barrier(
        (up_2, down_2, behind, wrap, cross)
    )
    mine, behind = join(flags, wrap, cross, behind, a, b, up, up_2, up_2, down_2, down_2, down)
    other = lax.ppermute(mine, "row", [(i, i ^ 1) for i in range(n_row)])
    sums, found = multiply(0, flags, om, tile, behind, mine)
    return multiply(1, flags, om, tile, behind, other, found, sums)[0]


def solution(mesh):
    step = functools.partial(local, n_row=mesh.shape["row"], n_col=mesh.shape["col"])
    return jax.shard_map(
        step,
        mesh=mesh,
        in_specs=(P("col", "row", None), P("col", "row"), P("col", "row")),
        out_specs=P("col", "row", None),
        check_vma=False,
    )
```
